32 devices in a mesh: res: 4 (over x, core), blk: 8 (over z, y).
Axes of the slice: x: 2, y: 2, z: 4, core: 2. Of those that a mesh axis runs over, the one named last changes fastest.
Arguments:
- modes: float32 [2, 8, 4194304], P(None, 'res', 'blk'), may hold values from -0.078125 to 0.078125
Outputs:
- product_modes: float32 [2, 8, 4194304], P(None, 'res', 'blk')
The draws below stay inside these ranges and needn't reach their ends.
All inputs are finite; a program needn't handle non-finite values.
Results may differ from the reference program's by a relative error of at most 0.000098.
Values sent between devices are 32-bit elements; how exact they have to be, the bound alone decides.
A program may use at most 192 MiB of HBM per device.

```python
import jax
import jax.numpy as jnp

MODES = 33554432
EIGHTH = 4194304
PADDED = 50331648


def block_levels(key, extent, cuts, smallest, largest):
    gain, own = 1.0, jax.random.fold_in(key, 6)
    for dim, blocks in cuts:
        heights = jnp.exp(jax.random.uniform(jax.random.fold_in(own, dim), (blocks,), jnp.float32, smallest / len(cuts), largest / len(cuts)))
        gain = gain * jnp.repeat(heights, extent[dim] // blocks).reshape([-1 if axis == dim else 1 for axis in range(len(extent))])
    return gain


def gaussian(own_key, dims, scale, most, shards=(), dtype=jnp.bfloat16):
    loudness = block_levels(own_key, dims, shards, -0.22, 0.18) if shards else 1.0
    values = jax.random.normal(own_key, dims, jnp.float32) * scale * loudness
    return jnp.minimum(jnp.maximum(values, -most), most).astype(dtype)


def setup_inputs(seed: int = 0) -> dict:
    key_of = jax.random.split(jax.random.key(seed), 2)
    modes = gaussian(key_of[0], (2, 8, EIGHTH), (MODES ** -0.25), 0.078125, ((1, 4), (2, 8)), jnp.float32)
    return {"modes": modes}


def reference(modes):
    series = (modes[0] + 1j * modes[1]).reshape(MODES)
    padded = jnp.pad(series, (0, PADDED - MODES))
    physical = jnp.fft.ifft(padded) * PADDED
    spectrum = jnp.fft.fft(physical * physical) / PADDED
    kept = spectrum[MODES // 2: MODES // 2 + MODES]
    result = jnp.stack([jnp.real(kept), jnp.imag(kept)]).reshape(2, 8, EIGHTH)
    return result.astype(jnp.float32)
```

```python
import math

import jax
import jax.numpy as jnp
from jax import lax
from jax.sharding import PartitionSpec as P

INNER = 512

high = lax.Precision.HIGH


def turn(numerator, period):
    angle = 2.0 * math.pi / period * (numerator % period).astype(jnp.float32)
    return jnp.cos(angle), jnp.sin(angle)


def times(left, right):
    return (left[0] * right[0] - left[1] * right[1], left[0] * right[1] + left[1] * right[0])


def conj(pair):
    return (pair[0], -pair[1])


def gauss_tables(length, zero):
    rows = lax.broadcasted_iota(jnp.int32, (length, length), 0) + zero
    columns = lax.broadcasted_iota(jnp.int32, (length, length), 1)
    cosine, sine = turn(rows * columns, length)
    return cosine, sine + cosine, sine - cosine


def dot(left, right):
    return jnp.dot(left, right, precision=high)


def forward_dft(multiply, tables, value):
    base = multiply(tables[0], value[0] + value[1])
    return (base - multiply(tables[1], value[1]), base + multiply(tables[2], value[0]))


def backward_dft(multiply, tables, value):
    base = multiply(tables[0], value[0] + value[1])
    return (base + multiply(tables[2], value[1]), base - multiply(tables[1], value[0]))


def from_left(table, value):
    return dot(table, value)


def from_right(table, value):
    return dot(value, table)


def on_device(modes):
    own, width = modes.shape[1:]
    blocks = lax.axis_size("blk")
    residues = lax.axis_size("res")
    block = lax.axis_index("blk")
    residue = lax.axis_index("res")
    narrow = width // blocks
    inner = min(INNER, width // 8)
    outer = width // inner
    eighths = own * residues
    period = residues * 3 * blocks
    padded = period * width
    zero = residue // (16 * residues)

    def swap(value, bit):
        return lax.ppermute(value, "res", [(q, q ^ bit) for q in range(residues)])

    def sections(owners, offset):
        shape = (3, blocks, 2, len(owners), 2, own, blocks)
        ids = [lax.broadcasted_iota(jnp.int32, shape, i) for i in range(7)]
        owner = sum(
            jnp.where(ids[3] == i, o, 0) for i, o in enumerate(owners)
        )
        freq = residues * (3 * ids[1] + ids[0]) + residue
        place = (own * owner + ids[5] + offset) * blocks + ids[6]
        cosine, sine = turn(freq * place, period)
        return jnp.where(ids[2] == ids[4], cosine, jnp.where(ids[2] == 0, -sine, sine))

    outer_tables = gauss_tables(outer, zero)
    inner_tables = gauss_tables(inner, zero)
    row_ids = lax.broadcasted_iota(jnp.int32, (outer, 1), 0) + zero
    column_ids = lax.broadcasted_iota(jnp.int32, (1, inner), 1)
    inner_turn = turn(row_ids * column_ids, width)

    moved_in = lax.all_to_all(
        modes.reshape(2, own, blocks, narrow), "blk", split_axis=2, concat_axis=2, tiled=True
    )
    mine = moved_in.reshape(2 * own * blocks, narrow)
    across = swap(mine, 2)
    beside = swap(mine, 1)
    diagonal = swap(across, 1)
    every = jnp.concatenate([mine, beside, across, diagonal], axis=0)
    order = [residue, residue ^ 1, residue ^ 2, residue ^ 3]
    matrix = sections(order, 0).reshape(3, 2 * blocks, 2 * own * blocks * residues)

    returned = []
    for slab in range(3):
        section = dot(matrix[slab], every).reshape(blocks, 2, narrow // 128, 128)
        back = lax.all_to_all(section, "blk", split_axis=0, concat_axis=0, tiled=True)
        local = (back[:, 0].reshape(outer, inner), back[:, 1].reshape(outer, inner))
        freq = residues * (3 * block + slab) + residue
        row_turn = turn(freq * (inner * row_ids), padded)
        column_turn = turn(freq * column_ids, padded)
        local = times(row_turn, times(column_turn, local))
        local = forward_dft(from_left, outer_tables, local)
        local = times(inner_turn, local)
        local = forward_dft(from_right, inner_tables, local)
        local = (local[0] * local[0] - local[1] * local[1], 2.0 * local[0] * local[1])
        local = backward_dft(from_right, inner_tables, local)
        local = times(conj(inner_turn), local)
        local = backward_dft(from_left, outer_tables, local)
        local = times(conj(row_turn), times(conj(column_turn), local))
        packed = jnp.stack(
            [part.reshape(blocks, narrow // 128, 128) for part in local], axis=1
        )
        moved = lax.all_to_all(packed, "blk", split_axis=0, concat_axis=0, tiled=True)
        returned.append(moved.reshape(2 * blocks, narrow))
    spectrum = jnp.concatenate(returned, axis=0)

    def share(owners):
        table = sections(owners, eighths // 2) * (1.0 / padded)
        table = table.reshape(6 * blocks, 2 * own * blocks * len(owners))
        return lax.dot_general(
            table, spectrum, (((0,), (0,)), ((), ())), precision=high
        )

    half = 2 * own * blocks
    given = swap(share([residue ^ 1, residue ^ 3]), 1)
    kept = share([residue, residue ^ 2])
    given_across = swap(kept[half:] + given[half:], 2)
    total = kept[:half] + given[:half] + given_across
    home = lax.all_to_all(
        total.reshape(2, own, blocks, narrow), "blk", split_axis=2, concat_axis=2, tiled=True
    )
    return home.reshape(2, own, width)


def solution(mesh):
    return jax.shard_map(
        on_device,
        mesh=mesh,
        in_specs=(P(None, "res", "blk"),),
        out_specs=P(None, "res", "blk"),
        check_vma=False,
    )
```
